256 devices in a mesh: ens: 4 (over z_hi, core), grid: 64 (over y, x, z_lo).
Axes of the slice: x: 4, y: 4, z: 8 (z_hi: 2, z_lo: 4; z = z_hi * 4 + z_lo), core: 2. Of those that a mesh axis runs over, the one named last changes fastest.
Arguments:
- embeddings: bfloat16 [8, 8192, 1024], P('ens', 'grid'), may hold values from -20 to 20
- reference_analysis: float32 [100, 8192], P(None, 'grid'), may hold values from -6 to 6
- attention_matrix: bfloat16 [1024, 3072], replicated, may hold values from -8 to 8
- readout_matrix: bfloat16 [1024, 100], replicated, may hold values from -0.1875 to 0.1875
- adjacent_blocks: int32 [128, 3], P('grid'), may hold values from 0 to 127, as said below
- companion_matrix: int32 [7, 8], replicated, may hold values from 0 to 7, as said below
- continent_indicator: int32 [8192], P('grid'), may hold values 0 or 1
- zonal_strip: int32 [8192], P('grid'), may hold values from 0 to 720
Outputs:
- energy_objective: float32 [], replicated
- embedding_sensitivity: float32 [8, 8192, 1024], P('ens', 'grid')
- grad_value_matrix: float32 [1048576], P(('ens', 'grid'))
- grad_dec: float32 [102400], P(('ens', 'grid'))
The draws below stay inside these ranges and needn't reach their ends.
Inputs may be any that keep to these rules, and one draw needn't show every extreme that they name: `adjacent_blocks`: entry 0 of row b is b; entry 1 lies 1 to 2 blocks before b and entry 2 lies 1 to 2 blocks after b, each clamped into 0 to 127. Each row is a perfect matching of the members: companion_matrix[r, companion_matrix[r, m]] = m and companion_matrix[r, m] != m; every two members are partners in exactly one row.
All inputs are finite; a program needn't handle non-finite values. No bound on the sum of `continent_indicator` on one device may be relied on, other than what follows from the above.
Results may differ from the reference program's by a relative error of at most 0.012.
The reference program's roundings to bfloat16 on the way count: a program that leaves them out, or rounds other values in their place, can miss the bound.
Values may be sent and summed in bfloat16 or wider, within the bound.
No kernel may reach another device: no remote copies, remote signals or barrier semaphores. Data moves between devices by JAX's collectives and lax.ppermute only.
A program may use at most 128 MiB of HBM per device.

```python
import math
import jax
import jax.numpy as jnp
from jax import lax

D = 1024
HEADS = 16
CH = 100
QB = 64
R_BLK = 2
NB = 3
SCORED_ENTRIES = 128
NLAT = 721
MEMBERS = 8
ROUNDS = 7
NPTS = 8192
NBLOCKS = 128


def draw_embeddings(key, part):
    array_shape = (MEMBERS, NPTS, D)
    values = jax.random.normal(jax.random.fold_in(key, 1), array_shape, jnp.float32)
    return jnp.clip(values, -20.0, 20.0).astype(jnp.bfloat16)


def draw_attention_matrix(key, part):
    values = jnp.clip(jax.random.normal(jax.random.fold_in(key, 1), (D, 3 * D), jnp.float32), -6.0, 6.0) / math.sqrt(D)
    return jnp.clip(values, -8.0, 8.0).astype(jnp.bfloat16)


def draw_adjacent_blocks(key, part):
    blocks = jnp.arange(NBLOCKS, dtype=jnp.int32)
    back_steps = jax.random.randint(jax.random.fold_in(key, 1), (NBLOCKS,), 1, R_BLK + 1, dtype=jnp.int32)
    ahead_steps = jax.random.randint(jax.random.fold_in(key, 2), (NBLOCKS,), 1, R_BLK + 1, dtype=jnp.int32)
    before = jnp.clip(blocks - back_steps, 0, NBLOCKS - 1)
    after = jnp.clip(blocks + ahead_steps, 0, NBLOCKS - 1)
    return jnp.stack([blocks, before, after], axis=1).astype(jnp.int32)


def draw_companion_matrix(key, part):
    relabel = jax.random.permutation(jax.random.fold_in(key, 1), MEMBERS).astype(jnp.int32)
    order = jax.random.permutation(jax.random.fold_in(key, 2), ROUNDS).astype(jnp.int32)
    inverse = jnp.argsort(relabel, stable=True).astype(jnp.int32)
    seats = inverse[None, :]
    round_ids = order[:, None]
    last_seat = MEMBERS - 1
    facing = jnp.mod(2 * round_ids - seats, last_seat)
    partner_seat = jnp.where(seats == last_seat, round_ids, jnp.where(seats == round_ids, last_seat, facing))
    return relabel[partner_seat].astype(jnp.int32)


def set_ends(entries, own_key, least, largest):
    index_at = [jax.random.randint(jax.random.fold_in(own_key, axis), (), 0, length) for axis, length in enumerate(entries.shape)]
    longest = entries.shape.index(max(entries.shape))
    next_to = index_at[:longest] + [(index_at[longest] + 1) % entries.shape[longest]] + index_at[longest + 1:]
    return entries.at[tuple(index_at)].set(least).at[tuple(next_to)].set(largest)


def steps_of(key, shape, shards, smallest, largest):
    def one(position, blocks):
        heights = jax.random.uniform(jax.random.fold_in(jax.random.fold_in(key, 6), position), (blocks,), jnp.float32, smallest / len(shards), largest / len(shards))
        return jnp.repeat(jnp.exp(heights), shape[position] // blocks).reshape((-1,) + (1,) * (len(shape) - position - 1))

    factor_of = one(*shards[0])
    for cut in shards[1:]:
        factor_of = factor_of * one(*cut)
    return factor_of


def gaussian(stream_key, extent, spread, reach, cuts=(), kind=jnp.bfloat16):
    result = jax.random.normal(stream_key, extent, jnp.float32) * spread
    if len(cuts) > 0:
        result = steps_of(stream_key, extent, cuts, -0.22, 0.18) * result
    return jnp.clip(result, min=-reach, max=reach).astype(kind)


def setup_inputs(seed: int = 0) -> dict:
    streams_of = jax.random.split(jax.random.key(seed), 9)
    embeddings = draw_embeddings(jax.random.fold_in(streams_of[8], 71), 0)
    reference_analysis = gaussian(streams_of[1], (CH, NPTS), 1.0, 6.0, ((1, 64),), jnp.float32)
    attention_matrix = draw_attention_matrix(jax.random.fold_in(streams_of[8], 71), 0)
    readout_matrix = gaussian(streams_of[3], (D, CH), D ** -0.5, 0.1875)
    adjacent_blocks = draw_adjacent_blocks(jax.random.fold_in(streams_of[8], 71), 0)
    companion_matrix = draw_companion_matrix(jax.random.fold_in(streams_of[8], 71), 0)
    continent_indicator = set_ends((jax.random.randint(streams_of[6], (NPTS,), 0, 10) < 3).astype(jnp.int32), jax.random.fold_in(streams_of[6], 1), 0, 1)
    zonal_strip = set_ends(jax.random.randint(streams_of[7], (NPTS,), 0, NLAT), jax.random.fold_in(streams_of[7], 1), 0, NLAT - 1).astype(jnp.int32)
    return dict(embeddings=embeddings, reference_analysis=reference_analysis, attention_matrix=attention_matrix, readout_matrix=readout_matrix, adjacent_blocks=adjacent_blocks, companion_matrix=companion_matrix, continent_indicator=continent_indicator, zonal_strip=zonal_strip)


EPSILON = 1e-06

def rms_scale(values):
    return lax.rsqrt(lax.optimization_barrier(jnp.mean(values * values, axis=-1, keepdims=True)) + EPSILON)

def sample_evaluate(embedded_grid, attention_matrix, readout_matrix, adjacent_blocks):
    block_count = embedded_grid.shape[0] // QB
    model_width = embedded_grid.shape[1]
    head_dim = model_width // HEADS
    score_scale = 1.0 / math.sqrt(head_dim)
    lat_float = embedded_grid.astype(jnp.float32)
    inv_first = rms_scale(lat_float)
    normed = (lat_float * inv_first).astype(jnp.bfloat16)
    projected = jnp.dot(normed, attention_matrix, preferred_element_type=jnp.float32).astype(jnp.bfloat16)
    queries = projected[:, :model_width].reshape(block_count, QB, HEADS, head_dim)
    keyval = projected[:, model_width:].reshape(block_count, QB, 2 * model_width)
    picked = keyval[adjacent_blocks.reshape(-1)].reshape(block_count, NB * QB, 2, HEADS, head_dim)
    window_keys = picked[:, :, 0]
    window_values = picked[:, :, 1]
    scores = jnp.einsum('bqhe,bkhe->bhqk', queries.astype(jnp.float32), window_keys.astype(jnp.float32)) * score_scale
    highest = lax.optimization_barrier(jnp.max(scores, axis=-1, keepdims=True))
    exp_scores = jnp.exp(scores - highest)
    attention = exp_scores / lax.optimization_barrier(jnp.sum(exp_scores, axis=-1, keepdims=True))
    attention16 = attention.astype(jnp.bfloat16)
    attended = jnp.einsum('bhqk,bkhe->bqhe', attention16.astype(jnp.float32), window_values.astype(jnp.float32))
    residual_state = lat_float + attended.reshape(embedded_grid.shape[0], model_width)
    inv_second = rms_scale(residual_state)
    internal_activation = (residual_state * inv_second).astype(jnp.bfloat16)
    predicted_grid = lax.dot_general(readout_matrix, internal_activation, (((0,), (1,)), ((), ())), preferred_element_type=jnp.float32)
    retained_entries = (lat_float, inv_first, normed, queries, window_keys, window_values, attention, attention16, residual_state, inv_second, internal_activation)
    return (predicted_grid, retained_entries)

def objective_factors(predicted_grids, reference_analysis, companion_matrix, continent_indicator, zonal_strip):
    sample_count, variable_indices, location_count = predicted_grids.shape
    region_count = location_count // SCORED_ENTRIES
    phase = (zonal_strip.astype(jnp.float32) + 0.5) * (math.pi / NLAT) - 0.5 * math.pi
    location_factors = (jnp.cos(phase) * (1.0 + continent_indicator.astype(jnp.float32))).reshape(region_count, SCORED_ENTRIES)
    region_sequence = predicted_grids.reshape(sample_count, variable_indices, region_count, SCORED_ENTRIES)
    target_patches = reference_analysis.reshape(variable_indices, region_count, SCORED_ENTRIES)
    error_component = region_sequence - target_patches[None]
    observed_separation = jnp.sqrt(lax.optimization_barrier(jnp.sum(location_factors * error_component * error_component, axis=-1)) + EPSILON)
    round_of = (jnp.arange(variable_indices, dtype=jnp.int32)[:, None] + jnp.arange(region_count, dtype=jnp.int32)[None, :]) % ROUNDS
    partner = jnp.transpose(companion_matrix[round_of], (2, 0, 1))
    partner_pick = (partner[..., None] == jnp.arange(sample_count, dtype=jnp.int32)).astype(jnp.float32)
    partner_patches = jnp.einsum('mcjn,ncjp->mcjp', partner_pick, region_sequence, precision=lax.Precision.HIGHEST)
    dispersion_component = region_sequence - partner_patches
    mutual_separation = jnp.sqrt(lax.optimization_barrier(jnp.sum(location_factors * dispersion_component * dispersion_component, axis=-1)) + EPSILON)
    total = jnp.sum(observed_separation) - 0.5 * jnp.sum(mutual_separation)
    energy_objective = total / (sample_count * variable_indices * region_count)
    predicted_sensitivity = location_factors * error_component / observed_separation[..., None] - location_factors * dispersion_component / mutual_separation[..., None]
    return (energy_objective, predicted_sensitivity.reshape(sample_count, variable_indices, location_count))

def sample_reverse(embedded_grid, predicted_sensitivity, attention_matrix, readout_matrix, adjacent_blocks):
    predicted_grid, retained_entries = sample_evaluate(embedded_grid, attention_matrix, readout_matrix, adjacent_blocks)
    lat_float, inv_first, normed, queries, window_keys, window_values, attention, attention16, residual_state, inv_second, internal_activation = retained_entries
    location_count, model_width = embedded_grid.shape
    block_count = location_count // QB
    head_dim = model_width // HEADS
    score_scale = 1.0 / math.sqrt(head_dim)
    sensitivity_reduced16 = predicted_sensitivity.astype(jnp.bfloat16)
    grad_dec = lax.dot_general(internal_activation, sensitivity_reduced16, (((0,), (1,)), ((), ())), preferred_element_type=jnp.float32)
    grad_hidden = lax.dot_general(sensitivity_reduced16, readout_matrix, (((0,), (1,)), ((), ())), preferred_element_type=jnp.float32)
    unit_state = residual_state * inv_second
    grad_state = inv_second * (grad_hidden - unit_state * lax.optimization_barrier(jnp.mean(grad_hidden * unit_state, axis=-1, keepdims=True)))
    grad_out16 = grad_state.astype(jnp.bfloat16).reshape(block_count, QB, HEADS, head_dim).astype(jnp.float32)
    grad_attention = jnp.einsum('bqhe,bkhe->bhqk', grad_out16, window_values.astype(jnp.float32))
    grad_values = jnp.einsum('bhqk,bqhe->bkhe', attention16.astype(jnp.float32), grad_out16)
    grad_scores = (attention * (grad_attention - lax.optimization_barrier(jnp.sum(attention * grad_attention, axis=-1, keepdims=True))) * score_scale).astype(jnp.bfloat16)
    grad_queries = jnp.einsum('bhqk,bkhe->bqhe', grad_scores.astype(jnp.float32), window_keys.astype(jnp.float32))
    grad_keys = jnp.einsum('bhqk,bqhe->bkhe', grad_scores.astype(jnp.float32), queries.astype(jnp.float32))
    grad_window = jnp.stack([grad_keys, grad_values], axis=2).reshape(block_count * NB, QB, 2 * model_width)
    gathered_back = jax.ops.segment_sum(grad_window, adjacent_blocks.reshape(-1), num_segments=block_count)
    grad_proj = jnp.concatenate([grad_queries.reshape(location_count, model_width), gathered_back.reshape(location_count, 2 * model_width)], axis=-1).astype(jnp.bfloat16)
    grad_value_matrix = lax.dot_general(normed, grad_proj[:, 2 * model_width:], (((0,), (0,)), ((), ())), preferred_element_type=jnp.float32)
    grad_normed = lax.dot_general(grad_proj, attention_matrix, (((1,), (1,)), ((), ())), preferred_element_type=jnp.float32)
    unit_input = lat_float * inv_first
    grad_latent = grad_state + inv_first * (grad_normed - unit_input * lax.optimization_barrier(jnp.mean(grad_normed * unit_input, axis=-1, keepdims=True)))
    return (grad_latent, grad_value_matrix, grad_dec)

def reference(embeddings, reference_analysis, attention_matrix, readout_matrix, adjacent_blocks, companion_matrix, continent_indicator, zonal_strip):

    def evaluation_only(embedded_grid):
        return sample_evaluate(embedded_grid, attention_matrix, readout_matrix, adjacent_blocks)[0]
    predicted_grids = lax.map(evaluation_only, embeddings)
    energy_objective, predicted_sensitivity = objective_factors(predicted_grids, reference_analysis, companion_matrix, continent_indicator, zonal_strip)

    def reverse_only(inputs):
        return sample_reverse(inputs[0], inputs[1], attention_matrix, readout_matrix, adjacent_blocks)
    embedding_sensitivity, value_factors, readout_factors = lax.map(reverse_only, (embeddings, predicted_sensitivity))
    return (energy_objective, embedding_sensitivity, lax.optimization_barrier(jnp.sum(value_factors, axis=0)).reshape(-1), lax.optimization_barrier(jnp.sum(readout_factors, axis=0)).reshape(-1))
```

```python
import math

import jax
import jax.numpy as jnp
from jax import lax
from jax.experimental import pallas as pl
from jax.experimental.pallas import tpu as pltpu
from jax.sharding import PartitionSpec as P

HEADS = 16
QB = 64
R_BLK = 2
NB = 3
SCORED_ENTRIES = 128
NLAT = 721
EPSILON = 1e-06

BF = jnp.bfloat16
F32 = jnp.float32
LANES = 128
GROUP = 256
BOTH = ("ens", "grid")

STRIDES = {"zh": (2, 128), "co": (2, 64), "y": (4, 16), "x": (4, 4), "zl": (4, 1)}
REDUCE_ORDER = ("co", "x", "y", "zh", "zl")


def nn(a, b):
    return lax.dot_general(a, b, (((1,), (0,)), ((), ())), preferred_element_type=F32)


def nt(a, b):
    return lax.dot_general(a, b, (((1,), (1,)), ((), ())), preferred_element_type=F32)


def tn(a, b):
    return lax.dot_general(a, b, (((0,), (0,)), ((), ())), preferred_element_type=F32)


def rms_scale(values):
    return lax.rsqrt(jnp.mean(values * values, axis=-1, keepdims=True) + EPSILON)


def normalised(rows):
    values = rows.astype(F32)
    return (values * rms_scale(values)).astype(BF)


def head_mask(dtype, head_dim):
    row = lax.broadcasted_iota(jnp.int32, (GROUP, GROUP), 0) // QB
    lane = lax.broadcasted_iota(jnp.int32, (GROUP, GROUP), 1) // head_dim
    return (row == lane).astype(F32).astype(dtype)


def stacked(rows, mask):
    return jnp.concatenate([rows] * (GROUP // QB), axis=0) * mask


def unstacked(values, mask):
    kept = values * mask
    return kept[0:QB] + kept[QB : 2 * QB] + kept[2 * QB : 3 * QB] + kept[3 * QB : 4 * QB]


def state_gradient(grad_hidden, state):
    inv = rms_scale(state)
    unit = state * inv
    return unit, inv * (grad_hidden - unit * jnp.mean(grad_hidden * unit, axis=-1, keepdims=True))


def call(kernel, outs, ins, smem=0, scratch=(), name=None):
    specs = [pl.BlockSpec(memory_space=pltpu.SMEM)] * smem
    specs += [pl.BlockSpec(memory_space=pltpu.VMEM)] * (len(ins) - smem)
    return pl.pallas_call(
        kernel,
        out_shape=[jax.ShapeDtypeStruct(s, d) for s, d in outs],
        in_specs=specs,
        out_specs=[pl.BlockSpec(memory_space=pltpu.VMEM)] * len(outs),
        scratch_shapes=list(scratch),
        compiler_params=pltpu.CompilerParams(vmem_limit_bytes=56 * 1024 * 1024),
        name=name,
    )(*ins)


def own_projection(emb, w, q_out, kv_out):
    width = emb.shape[1]
    normed = normalised(emb[...])
    for c in range(0, width, 512):
        q_out[:, c : c + 512] = nn(normed, w[:, c : c + 512]).astype(BF)
    for c in range(0, 2 * width, 512):
        kv_out[:, c : c + 512] = nn(normed, w[:, width + c : width + c + 512]).astype(BF)


def halo_query(emb_p, emb_n, w, q_out):
    width = emb_p.shape[1]
    normed = normalised(jnp.concatenate([emb_p[...], emb_n[...]], axis=0))
    for c in range(0, width, 512):
        q_out[:, c : c + 512] = nn(normed, w[:, c : c + 512]).astype(BF)


def forward(slots, emb_p, emb_n, emb, q, kv, w, readout, kvx, state, send, lse_out, forecast):
    members = kvx.shape[0]
    width = emb.shape[1]
    points = emb.shape[0] // members
    blocks = points // QB
    head_dim = width // HEADS
    scale = 1.0 / math.sqrt(head_dim)
    per = GROUP // head_dim
    normed = normalised(jnp.concatenate([emb_p[...], emb_n[...]], axis=0))
    for c in range(0, 2 * width, 512):
        part = nn(normed, w[:, width + c : width + c + 512]).astype(BF)
        for m in range(members):
            lo = m * points
            kvx[m, 0:points, c : c + 512] = part[lo : lo + points]
            kvx[m, 2 * points : 3 * points, c : c + 512] = part[
                (members + m) * points : (members + m + 1) * points
            ]
            kvx[m, points : 2 * points, c : c + 512] = kv[lo : lo + points, c : c + 512]
    mask16 = head_mask(BF, head_dim)
    mask32 = head_mask(F32, head_dim)
    lane = lax.broadcasted_iota(jnp.int32, (QB, LANES), 1)
    for m in range(members):
        for b in range(blocks):
            row = m * points + b * QB
            starts = [pl.multiple_of(slots[b * NB + i] * QB, QB) for i in range(NB)]
            packed = jnp.zeros((QB, LANES), F32)
            for u in range(width // GROUP):
                lanes = slice(u * GROUP, (u + 1) * GROUP)
                vlanes = slice(width + u * GROUP, width + (u + 1) * GROUP)
                qs = stacked(q[row : row + QB, lanes], mask16)
                kw = jnp.concatenate([kvx[m, pl.ds(s, QB), lanes] for s in starts], axis=0)
                vw = jnp.concatenate([kvx[m, pl.ds(s, QB), vlanes] for s in starts], axis=0)
                scores = nt(qs, kw) * scale
                top = jnp.max(scores, axis=-1, keepdims=True)
                exps = jnp.exp(scores - top)
                total = jnp.sum(exps, axis=-1, keepdims=True)
                attention16 = (exps / total).astype(BF)
                attended = unstacked(nn(attention16, vw), mask32)
                state[row : row + QB, lanes] = emb[row : row + QB, lanes].astype(F32) + attended
                send[row : row + QB, lanes] = attended.astype(BF)
                lse = top + jnp.log(total)
                for h in range(per):
                    packed = jnp.where(
                        lane % HEADS == u * per + h, lse[h * QB : (h + 1) * QB], packed
                    )
            lse_out[row : row + QB, :] = packed
            high = packed.astype(BF).astype(F32)
            rest = packed - high
            mid = rest.astype(BF).astype(F32)
            low = rest - mid
            pieces = jnp.where(
                lane < HEADS, high, jnp.where(lane < 2 * HEADS, mid, low)
            )
            send[row : row + QB, width : width + LANES] = pieces.astype(BF)
    values = state[...]
    hidden = (values * rms_scale(values)).astype(BF)
    forecast[...] = nn(hidden, readout[...])


def loss(own, every, truth, weight, partner, grad, total):
    points = truth.shape[0]
    members = own.shape[0] // points
    count = every.shape[0] // points
    lane = lax.broadcasted_iota(jnp.int32, (1, LANES), 1)
    w = weight[...]
    summed = jnp.zeros((1, LANES), F32)
    for m in range(members):
        mine = own[m * points : (m + 1) * points, :]
        ids = partner[m : m + 1, :]
        other = jnp.zeros_like(mine)
        for n in range(count):
            other = jnp.where(ids == n, every[n * points : (n + 1) * points, :], other)
        error = mine - truth[...]
        apart = mine - other
        d_truth = jnp.sqrt(jnp.sum(w * error * error, axis=0, keepdims=True) + EPSILON)
        d_pair = jnp.sqrt(jnp.sum(w * apart * apart, axis=0, keepdims=True) + EPSILON)
        grad[m * points : (m + 1) * points, :] = (
            w * error / d_truth - w * apart / d_pair
        ).astype(BF)
        summed = summed + d_truth - 0.5 * d_pair
    channels = partner[members : members + 1, :]
    value = jnp.sum(jnp.where(lane < channels, summed, 0.0), axis=-1, keepdims=True)
    total[...] = jnp.broadcast_to(value, total.shape)


def row_groups():
    pairs = []
    for zh in range(2):
        for co in range(2):
            for y in range(4):
                for x in range(4):
                    source = zh * 32 + co * 16 + y * 4 + x
                    target = co * 32 + x * 8 + y * 2 + zh
                    pairs.append((source * 16, target * 16))
    return pairs


def own_backward(
    slots, grad, state, readout, q, kvx, lse, total, grad_state, dec, grad_q, dkv, acc
):
    members = kvx.shape[0]
    width = state.shape[1]
    points = state.shape[0] // members
    blocks = points // QB
    head_dim = width // HEADS
    scale = 1.0 / math.sqrt(head_dim)
    per = GROUP // head_dim
    channels = 100
    grad_hidden = nt(grad[...], readout[...])
    unit, gs = state_gradient(grad_hidden, state[...])
    grad_state[...] = gs
    dec_part = tn(unit.astype(BF), grad[...])
    lane = lax.broadcasted_iota(jnp.int32, dec_part.shape, 1)
    dec_part = jnp.where(lane < channels, dec_part, total[0:1, :])
    for source, target in row_groups():
        dec[target : target + 16, :] = dec_part[source : source + 16, :]
    acc[...] = jnp.zeros_like(acc)
    mask16 = head_mask(BF, head_dim)
    mask32 = head_mask(F32, head_dim)
    for m in range(members):
        for b in range(blocks):
            row = m * points + b * QB
            starts = [pl.multiple_of(slots[b * NB + i] * QB, QB) for i in range(NB)]
            for u in range(width // GROUP):
                lanes = slice(u * GROUP, (u + 1) * GROUP)
                vlanes = slice(width + u * GROUP, width + (u + 1) * GROUP)
                qs = stacked(q[row : row + QB, lanes], mask16)
                dos = stacked(grad_state[row : row + QB, lanes].astype(BF), mask16)
                kw = jnp.concatenate([kvx[m, pl.ds(s, QB), lanes] for s in starts], axis=0)
                vw = jnp.concatenate([kvx[m, pl.ds(s, QB), vlanes] for s in starts], axis=0)
                column = jnp.concatenate(
                    [lse[row : row + QB, u * per + h : u * per + h + 1] for h in range(per)],
                    axis=0,
                )
                attention = jnp.exp(nt(qs, kw) * scale - column)
                attention16 = attention.astype(BF)
                grad_att = nt(dos, vw)
                delta = jnp.sum(attention * grad_att, axis=-1, keepdims=True)
                grad_scores = (attention * (grad_att - delta) * scale).astype(BF)
                grad_q[row : row + QB, lanes] = unstacked(nn(grad_scores, kw), mask32).astype(BF)
                dk = tn(grad_scores, qs)
                dv = tn(attention16, dos)
                for i, s in enumerate(starts):
                    piece = slice(i * QB, (i + 1) * QB)
                    acc[m, pl.ds(s, QB), lanes] += dk[piece]
                    acc[m, pl.ds(s, QB), vlanes] += dv[piece]
    for m in range(members):
        dkv[m] = acc[m, points : 2 * points, :]


def halo_backward(
    targets, emb_p, emb_n, got_p, got_n, grad_p, grad_n, q_halo, kvx, readout, dkv_in, emb,
    grad_kv, value_part, go, acc,
):
    members = kvx.shape[0]
    width = emb.shape[1]
    points = emb.shape[0] // members
    blocks = points // QB
    head_dim = width // HEADS
    scale = 1.0 / math.sqrt(head_dim)
    per = GROUP // head_dim
    acc[...] = dkv_in[...]
    mask16 = head_mask(BF, head_dim)
    mask32 = head_mask(F32, head_dim)
    for side, (emb_s, got, grad) in enumerate(
        ((emb_p, got_p, grad_p), (emb_n, got_n, grad_n))
    ):
        state = emb_s[...].astype(F32) + got[:, :width].astype(F32)
        _, gs = state_gradient(nt(grad[...], readout[...]), state)
        go[...] = gs.astype(BF)
        for b in range(blocks):
            target = targets[side * blocks + b]

            @pl.when(target >= 0)
            def _(b=b, target=target, side=side, got=got):
                start = pl.multiple_of(target * QB, QB)
                window = pl.multiple_of(target * QB + points, QB)
                for m in range(members):
                    row = m * points + b * QB
                    stats = got[row : row + QB, width : width + LANES].astype(F32)
                    lse = (
                        stats[:, 0:HEADS]
                        + stats[:, HEADS : 2 * HEADS]
                        + stats[:, 2 * HEADS : 3 * HEADS]
                    )
                    for u in range(width // GROUP):
                        lanes = slice(u * GROUP, (u + 1) * GROUP)
                        vlanes = slice(width + u * GROUP, width + (u + 1) * GROUP)
                        qrow = side * members * points + row
                        qs = stacked(q_halo[qrow : qrow + QB, lanes], mask16)
                        do = go[row : row + QB, lanes]
                        dos = stacked(do, mask16)
                        prod = do.astype(F32) * got[row : row + QB, lanes].astype(F32)
                        delta = jnp.sum(stacked(prod, mask32), axis=-1, keepdims=True)
                        column = jnp.concatenate(
                            [lse[:, u * per + h : u * per + h + 1] for h in range(per)], axis=0
                        )
                        kt = kvx[m, pl.ds(window, QB), lanes]
                        vt = kvx[m, pl.ds(window, QB), vlanes]
                        attention = jnp.exp(nt(qs, kt) * scale - column)
                        grad_att = nt(dos, vt)
                        grad_scores = (attention * (grad_att - delta) * scale).astype(BF)
                        acc[m, pl.ds(start, QB), lanes] += tn(grad_scores, qs)
                        acc[m, pl.ds(start, QB), vlanes] += tn(attention.astype(BF), dos)

    for m in range(members):
        grad_kv[m * points : (m + 1) * points, :] = acc[m].astype(BF)
    normed = normalised(emb[...])
    part = tn(normed, grad_kv[:, width : 2 * width])
    for source, target in row_groups():
        value_part[target : target + 16, :] = part[source : source + 16, :].astype(BF)


def input_gradient(emb, grad_q, grad_kv, w, grad_state, out):
    width = emb.shape[1]
    x = emb[...].astype(F32)
    inv = rms_scale(x)
    unit = x * inv
    gn = nt(grad_q[...], w[:, :width]) + nt(grad_kv[...], w[:, width:])
    out[...] = grad_state[...] + inv * (
        gn - unit * jnp.mean(gn * unit, axis=-1, keepdims=True)
    )


def shifted(value, axis, steps):
    extent, stride = STRIDES[axis]
    moves = []
    for source in range(256):
        at = source // stride % extent
        moves.append((source, source + ((at + steps) % extent - at) * stride))
    return lax.ppermute(value, BOTH, moves)


def scattered(value, flat):
    for axis in REDUCE_ORDER:
        extent, stride = STRIDES[axis]
        at = flat // stride % extent
        pieces = value.reshape((extent, value.shape[0] // extent) + value.shape[1:])
        own = lax.dynamic_index_in_dim(pieces, at, 0, keepdims=False).astype(F32)
        for k in range(1, extent):
            piece = lax.dynamic_index_in_dim(pieces, (at + k) % extent, 0, keepdims=False)
            own = own + shifted(piece, axis, k).astype(F32)
        value = own.astype(value.dtype)
    return own


def per_device(
    embeddings,
    reference_analysis,
    attention_matrix,
    readout_matrix,
    adjacent_blocks,
    companion_matrix,
    continent_indicator,
    zonal_strip,
):
    members, points, width = embeddings.shape
    channels = reference_analysis.shape[0]
    rounds, count = companion_matrix.shape
    blocks = points // QB
    rows = members * points
    size = lax.axis_size("grid")
    place = lax.axis_index("grid")
    ens = lax.axis_index("ens")
    flat = ens * size + place
    up = [(i, i + 1) for i in range(size - 1)]
    down = [(j, i) for i, j in up]

    emb = embeddings.reshape(rows, width)
    emb_p = lax.ppermute(emb, "grid", up)
    emb_n = lax.ppermute(emb, "grid", down)
    adj_p = lax.ppermute(adjacent_blocks, "grid", up)
    adj_n = lax.ppermute(adjacent_blocks, "grid", down)
    first = place * blocks
    slots = (adjacent_blocks - first + R_BLK).reshape(-1)
    to_p = jnp.where(place > 0, adj_p[:, 2] - first, -1)
    to_n = jnp.where(place < size - 1, adj_n[:, 1] - first, -1)
    targets = jnp.concatenate([to_p, to_n])
    targets = jnp.where((targets >= 0) & (targets < blocks), targets, -1)

    readout = jnp.pad(readout_matrix, ((0, 0), (0, LANES - channels)))
    truth = jnp.pad(reference_analysis, ((0, LANES - channels), (0, 0))).T
    phase = (zonal_strip.astype(F32) + 0.5) * (math.pi / NLAT) - 0.5 * math.pi
    weight = jnp.cos(phase) * (1.0 + continent_indicator.astype(F32))
    weight = jnp.broadcast_to(weight[:, None], (points, LANES))
    round_of = (jnp.arange(LANES, dtype=jnp.int32) + place) % rounds
    own_ids = ens * members + jnp.arange(members, dtype=jnp.int32)
    own_pick = (jnp.arange(count, dtype=jnp.int32)[None, :] == own_ids[:, None]).astype(jnp.int32)
    own_partners = jnp.sum(companion_matrix[None] * own_pick[:, None, :], axis=-1)
    partner = jnp.zeros((members, LANES), jnp.int32)
    for r in range(rounds):
        partner = jnp.where(round_of[None, :] == r, own_partners[:, r : r + 1], partner)
    partner = jnp.concatenate(
        [partner, jnp.full((8 - members, LANES), channels, jnp.int32)], axis=0
    )

    q, kv = call(
        own_projection, [((rows, width), BF), ((rows, 2 * width), BF)],
        [emb, attention_matrix], name="own_projection",
    )
    kvx, state, send, lse, forecast = call(
        forward,
        [
            ((members, 3 * points, 2 * width), BF),
            ((rows, width), F32),
            ((rows, width + LANES), BF),
            ((rows, LANES), F32),
            ((rows, LANES), F32),
        ],
        [slots, emb_p, emb_n, emb, q, kv, attention_matrix, readout],
        smem=1, name="forward",
    )
    every = lax.all_gather(forecast, "ens", axis=0, tiled=True)
    got_p = lax.ppermute(send, "grid", up)
    got_n = lax.ppermute(send, "grid", down)
    (q_halo,) = call(
        halo_query, [((2 * rows, width), BF)], [emb_p, emb_n, attention_matrix], name="halo_query"
    )
    grad, total = call(
        loss, [((rows, LANES), BF), ((8, LANES), F32)],
        [forecast, every, truth, weight, partner], name="loss",
    )
    grad_p = lax.ppermute(grad, "grid", up)
    grad_n = lax.ppermute(grad, "grid", down)
    grad_state, dec, grad_q, dkv = call(
        own_backward,
        [
            ((rows, width), F32),
            ((width, LANES), F32),
            ((rows, width), BF),
            ((members, points, 2 * width), F32),
        ],
        [slots, grad, state, readout, q, kvx, lse, total],
        smem=1,
        scratch=[pltpu.VMEM((members, 3 * points, 2 * width), F32)],
        name="own_backward",
    )
    dec_own = scattered(dec, flat)
    grad_kv, value_part = call(
        halo_backward,
        [((rows, 2 * width), BF), ((width, width), BF)],
        [targets, emb_p, emb_n, got_p, got_n, grad_p, grad_n, q_halo, kvx, readout, dkv, emb],
        smem=1,
        scratch=[pltpu.VMEM((rows, width), BF), pltpu.VMEM((members, points, 2 * width), F32)],
        name="halo_backward",
    )
    value_own = scattered(value_part, flat)
    (sensitivity,) = call(
        input_gradient, [((rows, width), F32)],
        [emb, grad_q, grad_kv, attention_matrix, grad_state], name="input_gradient",
    )
    energy = dec_own[0, channels] / (count * channels * size * (points // SCORED_ENTRIES))
    return (
        energy,
        sensitivity.reshape(members, points, width),
        value_own.reshape(-1),
        dec_own[:, :channels].reshape(-1),
    )


def solution(mesh):
    in_specs = (
        P("ens", "grid", None),
        P(None, "grid"),
        P(),
        P(),
        P("grid", None),
        P(),
        P("grid"),
        P("grid"),
    )
    out_specs = (P(), P("ens", "grid", None), P(("ens", "grid")), P(("ens", "grid")))
    return jax.shard_map(
        per_device, mesh=mesh, in_specs=in_specs, out_specs=out_specs, check_vma=False
    )
```

```python
import math

import jax
import jax.numpy as jnp
from jax import lax
from jax.experimental import pallas as pl
from jax.experimental.pallas import tpu as pltpu
from jax.sharding import PartitionSpec as P

HEADS = 16
QB = 64
R_BLK = 2
NB = 3
SCORED_ENTRIES = 128
NLAT = 721
EPSILON = 1e-06

BF = jnp.bfloat16
F32 = jnp.float32
LANES = 128
GROUP = 256
BOTH = ("ens", "grid")

STRIDES = {"zh": (2, 128), "co": (2, 64), "y": (4, 16), "x": (4, 4), "zl": (4, 1)}


def nn(a, b):
    return lax.dot_general(a, b, (((1,), (0,)), ((), ())), preferred_element_type=F32)


def nt(a, b):
    return lax.dot_general(a, b, (((1,), (1,)), ((), ())), preferred_element_type=F32)


def tn(a, b):
    return lax.dot_general(a, b, (((0,), (0,)), ((), ())), preferred_element_type=F32)


def rms_scale(values):
    return lax.rsqrt(jnp.mean(values * values, axis=-1, keepdims=True) + EPSILON)


def normalised(rows):
    values = rows.astype(F32)
    return (values * rms_scale(values)).astype(BF)


def head_mask(dtype, head_dim):
    row = lax.broadcasted_iota(jnp.int32, (GROUP, GROUP), 0) // QB
    lane = lax.broadcasted_iota(jnp.int32, (GROUP, GROUP), 1) // head_dim
    return (row == lane).astype(F32).astype(dtype)


def stacked(rows, mask):
    return jnp.concatenate([rows] * (GROUP // QB), axis=0) * mask


def unstacked(values, mask):
    kept = values * mask
    return kept[0:QB] + kept[QB : 2 * QB] + kept[2 * QB : 3 * QB] + kept[3 * QB : 4 * QB]


def state_gradient(grad_hidden, state):
    inv = rms_scale(state)
    unit = state * inv
    return unit, inv * (grad_hidden - unit * jnp.mean(grad_hidden * unit, axis=-1, keepdims=True))


def call(kernel, outs, ins, smem=0, scratch=(), name=None):
    specs = [pl.BlockSpec(memory_space=pltpu.SMEM)] * smem
    specs += [pl.BlockSpec(memory_space=pltpu.VMEM)] * (len(ins) - smem)
    return pl.pallas_call(
        kernel,
        out_shape=[jax.ShapeDtypeStruct(s, d) for s, d in outs],
        in_specs=specs,
        out_specs=[pl.BlockSpec(memory_space=pltpu.VMEM)] * len(outs),
        scratch_shapes=list(scratch),
        compiler_params=pltpu.CompilerParams(vmem_limit_bytes=56 * 1024 * 1024),
        name=name,
    )(*ins)


def own_projection(emb, w, q_out, kv_out):
    width = emb.shape[1]
    normed = normalised(emb[...])
    for c in range(0, width, 512):
        q_out[:, c : c + 512] = nn(normed, w[:, c : c + 512]).astype(BF)
    for c in range(0, 2 * width, 512):
        kv_out[:, c : c + 512] = nn(normed, w[:, width + c : width + c + 512]).astype(BF)


def halo_query(emb_p, emb_n, w, q_out):
    width = emb_p.shape[1]
    normed = normalised(jnp.concatenate([emb_p[...], emb_n[...]], axis=0))
    for c in range(0, width, 512):
        q_out[:, c : c + 512] = nn(normed, w[:, c : c + 512]).astype(BF)


def forward(slots, emb_p, emb_n, emb, q, kv, w, readout, kvx, state, send, lse_out, forecast):
    members = kvx.shape[0]
    width = emb.shape[1]
    points = emb.shape[0] // members
    blocks = points // QB
    head_dim = width // HEADS
    scale = 1.0 / math.sqrt(head_dim)
    per = GROUP // head_dim
    normed = normalised(jnp.concatenate([emb_p[...], emb_n[...]], axis=0))
    for c in range(0, 2 * width, 512):
        part = nn(normed, w[:, width + c : width + c + 512]).astype(BF)
        for m in range(members):
            lo = m * points
            kvx[m, 0:points, c : c + 512] = part[lo : lo + points]
            kvx[m, 2 * points : 3 * points, c : c + 512] = part[
                (members + m) * points : (members + m + 1) * points
            ]
            kvx[m, points : 2 * points, c : c + 512] = kv[lo : lo + points, c : c + 512]
    mask16 = head_mask(BF, head_dim)
    mask32 = head_mask(F32, head_dim)
    lane = lax.broadcasted_iota(jnp.int32, (QB, LANES), 1)

    def step(mb, carry):
        m, b = mb // blocks, mb % blocks
        row = pl.ds(pl.multiple_of(mb * QB, QB), QB)
        starts = [pl.multiple_of(slots[b * NB + i] * QB, QB) for i in range(NB)]
        packed = jnp.zeros((QB, LANES), F32)
        for u in range(width // GROUP):
            lanes = slice(u * GROUP, (u + 1) * GROUP)
            vlanes = slice(width + u * GROUP, width + (u + 1) * GROUP)
            qs = stacked(q[row, lanes], mask16)
            kw = jnp.concatenate([kvx[m, pl.ds(s, QB), lanes] for s in starts], axis=0)
            vw = jnp.concatenate([kvx[m, pl.ds(s, QB), vlanes] for s in starts], axis=0)
            scores = nt(qs, kw) * scale
            top = jnp.max(scores, axis=-1, keepdims=True)
            exps = jnp.exp(scores - top)
            total = jnp.sum(exps, axis=-1, keepdims=True)
            attention16 = (exps / total).astype(BF)
            attended = unstacked(nn(attention16, vw), mask32)
            state[row, lanes] = emb[row, lanes].astype(F32) + attended
            send[row, lanes] = attended.astype(BF)
            lse = top + jnp.log(total)
            for h in range(per):
                packed = jnp.where(
                    lane % HEADS == u * per + h, lse[h * QB : (h + 1) * QB], packed
                )
        lse_out[row, :] = packed
        high = packed.astype(BF).astype(F32)
        rest = packed - high
        mid = rest.astype(BF).astype(F32)
        pieces = jnp.where(lane < HEADS, high, jnp.where(lane < 2 * HEADS, mid, rest - mid))
        send[row, width : width + LANES] = pieces.astype(BF)
        return carry

    lax.fori_loop(0, members * blocks, step, 0)
    values = state[...]
    hidden = (values * rms_scale(values)).astype(BF)
    forecast[...] = nn(hidden, readout[...])


def loss(own, every, truth, weight, partner, grad, total):
    points = truth.shape[0]
    members = own.shape[0] // points
    count = every.shape[0] // points
    lane = lax.broadcasted_iota(jnp.int32, (1, LANES), 1)
    w = weight[...]
    summed = jnp.zeros((1, LANES), F32)
    for m in range(members):
        mine = own[m * points : (m + 1) * points, :]
        ids = partner[m : m + 1, :]
        other = jnp.zeros_like(mine)
        for n in range(count):
            other = jnp.where(ids == n, every[n * points : (n + 1) * points, :], other)
        error = mine - truth[...]
        apart = mine - other
        d_truth = jnp.sqrt(jnp.sum(w * error * error, axis=0, keepdims=True) + EPSILON)
        d_pair = jnp.sqrt(jnp.sum(w * apart * apart, axis=0, keepdims=True) + EPSILON)
        grad[m * points : (m + 1) * points, :] = (
            w * error / d_truth - w * apart / d_pair
        ).astype(BF)
        summed = summed + d_truth - 0.5 * d_pair
    channels = partner[members : members + 1, :]
    value = jnp.sum(jnp.where(lane < channels, summed, 0.0), axis=-1, keepdims=True)
    total[...] = jnp.broadcast_to(value, total.shape)


def row_groups():
    pairs = []
    for zh in range(2):
        for co in range(2):
            for y in range(4):
                for x in range(4):
                    source = zh * 32 + co * 16 + y * 4 + x
                    target = co * 32 + x * 8 + y * 2 + zh
                    pairs.append((source * 16, target * 16))
    return pairs


def columns(stats, u, per):
    return jnp.concatenate(
        [stats[:, u * per + h : u * per + h + 1] for h in range(per)], axis=0
    )


def own_values(
    slots, ids, grad, state, readout, q, kvx, lse, total, grad_state, dec, dv_out, acc
):
    members = kvx.shape[0]
    width = state.shape[1]
    points = state.shape[0] // members
    blocks = points // QB
    head_dim = width // HEADS
    scale = 1.0 / math.sqrt(head_dim)
    per = GROUP // head_dim
    unit, gs = state_gradient(nt(grad[...], readout[...]), state[...])
    grad_state[...] = gs
    dec_part = tn(unit.astype(BF), grad[...])
    channels, group = ids[0], ids[1]
    value = jnp.broadcast_to(total[0:1, :], dec_part.shape)
    lane = lax.broadcasted_iota(jnp.int32, dec_part.shape, 1)
    row = lax.broadcasted_iota(jnp.int32, dec_part.shape, 0)
    high = value.astype(BF).astype(F32)
    mid = (value - high).astype(BF).astype(F32)
    low = value - high - mid
    at = lane - channels - group % 8 * 3
    piece = jnp.where(at == 0, high, jnp.where(at == 1, mid, low))
    here = (at >= 0) & (at < 3) & (row % 4 == group // 8)
    dec_part = jnp.where(lane < channels, dec_part, jnp.where(here, piece, 0.0)).astype(BF)
    for source, target in row_groups():
        dec[target : target + 16, :] = dec_part[source : source + 16, :]
    acc[...] = jnp.zeros_like(acc)
    mask16 = head_mask(BF, head_dim)

    def step(mb, carry):
        m, b = mb // blocks, mb % blocks
        row = pl.ds(pl.multiple_of(mb * QB, QB), QB)
        starts = [pl.multiple_of(slots[b * NB + i] * QB, QB) for i in range(NB)]
        stats = lse[row, 0:HEADS]
        for u in range(width // GROUP):
            lanes = slice(u * GROUP, (u + 1) * GROUP)
            qs = stacked(q[row, lanes], mask16)
            dos = stacked(grad_state[row, lanes].astype(BF), mask16)
            kw = jnp.concatenate([kvx[m, pl.ds(s, QB), lanes] for s in starts], axis=0)
            attention = jnp.exp(nt(qs, kw) * scale - columns(stats, u, per))
            dv = tn(attention.astype(BF), dos)
            for i, s in enumerate(starts):
                acc[m, pl.ds(s, QB), lanes] += dv[i * QB : (i + 1) * QB]
        return carry

    lax.fori_loop(0, members * blocks, step, 0)
    for m in range(members):
        dv_out[m] = acc[m, points : 2 * points, :]


def summed_stats(stats):
    pieces = stats.astype(F32)
    return (
        pieces[:, 0:HEADS] + pieces[:, HEADS : 2 * HEADS] + pieces[:, 2 * HEADS : 3 * HEADS]
    )


def halo_values(
    targets, emb_p, emb_n, got_p, got_n, grad_p, grad_n, q_halo, kvx, readout, dv_in, emb, dec,
    go, grad_v, parts, acc,
):
    members = kvx.shape[0]
    rows, width = emb.shape
    points = rows // members
    blocks = points // QB
    head_dim = width // HEADS
    scale = 1.0 / math.sqrt(head_dim)
    per = GROUP // head_dim
    acc[...] = dv_in[...]
    mask16 = head_mask(BF, head_dim)
    for side, (emb_s, got, grad) in enumerate(
        ((emb_p, got_p, grad_p), (emb_n, got_n, grad_n))
    ):
        state = emb_s[...].astype(F32) + got[:, :width].astype(F32)
        _, gs = state_gradient(nt(grad[...], readout[...]), state)
        go[side * rows : (side + 1) * rows, :] = gs.astype(BF)

        def step(mb, carry, side=side, got=got):
            m, b = mb // blocks, mb % blocks
            target = targets[side * blocks + b]

            @pl.when(target >= 0)
            def _():
                row = pl.ds(pl.multiple_of(mb * QB, QB), QB)
                halo = pl.ds(pl.multiple_of(side * rows + mb * QB, QB), QB)
                start = pl.ds(pl.multiple_of(target * QB, QB), QB)
                window = pl.ds(pl.multiple_of(target * QB + points, QB), QB)
                stats = summed_stats(got[row, width : width + LANES])
                for u in range(width // GROUP):
                    lanes = slice(u * GROUP, (u + 1) * GROUP)
                    qs = stacked(q_halo[halo, lanes], mask16)
                    dos = stacked(go[halo, lanes], mask16)
                    kt = kvx[m, window, lanes]
                    attention = jnp.exp(nt(qs, kt) * scale - columns(stats, u, per))
                    acc[m, start, lanes] += tn(attention.astype(BF), dos)

            return carry

        lax.fori_loop(0, members * blocks, step, 0)
    for m in range(members):
        grad_v[m * points : (m + 1) * points, :] = acc[m].astype(BF)
    part = tn(normalised(emb[...]), grad_v[...]).astype(BF)
    for source, target in row_groups():
        parts[target : target + 16, 0:width] = part[source : source + 16, :]
    parts[:, width : width + LANES] = dec[...]


def score_backward(
    slots, targets, grad_state, q, kvx, lse, got_p, got_n, q_halo, go, grad_q, grad_k, acc
):
    members = kvx.shape[0]
    rows, width = grad_state.shape
    points = rows // members
    blocks = points // QB
    head_dim = width // HEADS
    scale = 1.0 / math.sqrt(head_dim)
    per = GROUP // head_dim
    acc[...] = jnp.zeros_like(acc)
    mask16 = head_mask(BF, head_dim)
    mask32 = head_mask(F32, head_dim)

    def own_step(mb, carry):
        m, b = mb // blocks, mb % blocks
        row = pl.ds(pl.multiple_of(mb * QB, QB), QB)
        starts = [pl.multiple_of(slots[b * NB + i] * QB, QB) for i in range(NB)]
        stats = lse[row, 0:HEADS]
        for u in range(width // GROUP):
            lanes = slice(u * GROUP, (u + 1) * GROUP)
            vlanes = slice(width + u * GROUP, width + (u + 1) * GROUP)
            qs = stacked(q[row, lanes], mask16)
            dos = stacked(grad_state[row, lanes].astype(BF), mask16)
            kw = jnp.concatenate([kvx[m, pl.ds(s, QB), lanes] for s in starts], axis=0)
            vw = jnp.concatenate([kvx[m, pl.ds(s, QB), vlanes] for s in starts], axis=0)
            attention = jnp.exp(nt(qs, kw) * scale - columns(stats, u, per))
            grad_att = nt(dos, vw)
            delta = jnp.sum(attention * grad_att, axis=-1, keepdims=True)
            grad_scores = (attention * (grad_att - delta) * scale).astype(BF)
            grad_q[row, lanes] = unstacked(nn(grad_scores, kw), mask32).astype(BF)
            dk = tn(grad_scores, qs)
            for i, s in enumerate(starts):
                acc[m, pl.ds(s, QB), lanes] += dk[i * QB : (i + 1) * QB]
        return carry

    lax.fori_loop(0, members * blocks, own_step, 0)
    for side, got in enumerate((got_p, got_n)):

        def step(mb, carry, side=side, got=got):
            m, b = mb // blocks, mb % blocks
            target = targets[side * blocks + b]

            @pl.when(target >= 0)
            def _():
                row = pl.ds(pl.multiple_of(mb * QB, QB), QB)
                halo = pl.ds(pl.multiple_of(side * rows + mb * QB, QB), QB)
                window = pl.ds(pl.multiple_of(target * QB + points, QB), QB)
                stats = summed_stats(got[row, width : width + LANES])
                for u in range(width // GROUP):
                    lanes = slice(u * GROUP, (u + 1) * GROUP)
                    vlanes = slice(width + u * GROUP, width + (u + 1) * GROUP)
                    qs = stacked(q_halo[halo, lanes], mask16)
                    do = go[halo, lanes]
                    prod = do.astype(F32) * got[row, lanes].astype(F32)
                    delta = jnp.sum(stacked(prod, mask32), axis=-1, keepdims=True)
                    kt = kvx[m, window, lanes]
                    vt = kvx[m, window, vlanes]
                    attention = jnp.exp(nt(qs, kt) * scale - columns(stats, u, per))
                    grad_att = nt(stacked(do, mask16), vt)
                    grad_scores = (attention * (grad_att - delta) * scale).astype(BF)
                    acc[m, window, lanes] += tn(grad_scores, qs)

            return carry

        lax.fori_loop(0, members * blocks, step, 0)
    for m in range(members):
        grad_k[m * points : (m + 1) * points, :] = acc[m, points : 2 * points, :].astype(BF)


def input_gradient(emb, grad_q, grad_k, grad_v, w, grad_state, out):
    width = emb.shape[1]
    x = emb[...].astype(F32)
    inv = rms_scale(x)
    unit = x * inv
    gn = nt(grad_q[...], w[:, :width]) + nt(grad_k[...], w[:, width : 2 * width])
    gn = gn + nt(grad_v[...], w[:, 2 * width :])
    out[...] = grad_state[...] + inv * (
        gn - unit * jnp.mean(gn * unit, axis=-1, keepdims=True)
    )


def shifted(value, axis, steps):
    extent, stride = STRIDES[axis]
    moves = []
    for source in range(256):
        at = source // stride % extent
        moves.append((source, source + ((at + steps) % extent - at) * stride))
    return lax.ppermute(value, BOTH, moves)


def scatter_start(value, flat, axis):
    extent, stride = STRIDES[axis]
    at = flat // stride % extent
    pieces = value.reshape((extent, value.shape[0] // extent) + value.shape[1:])
    got = []
    for k in range(1, extent):
        piece = lax.dynamic_index_in_dim(pieces, (at + k) % extent, 0, keepdims=False)
        got.append(shifted(piece, axis, k))
    return pieces, got


def scatter_end(pieces, got, flat, axis):
    extent, stride = STRIDES[axis]
    at = flat // stride % extent
    own = lax.dynamic_index_in_dim(pieces, at, 0, keepdims=False).astype(F32)
    for piece in got:
        own = own + piece.astype(F32)
    return own


def per_device(
    embeddings,
    reference_analysis,
    attention_matrix,
    readout_matrix,
    adjacent_blocks,
    companion_matrix,
    continent_indicator,
    zonal_strip,
):
    members, points, width = embeddings.shape
    channels = reference_analysis.shape[0]
    rounds, count = companion_matrix.shape
    blocks = points // QB
    rows = members * points
    size = lax.axis_size("grid")
    place = lax.axis_index("grid")
    ens = lax.axis_index("ens")
    flat = ens * size + place
    up = [(i, i + 1) for i in range(size - 1)]
    down = [(j, i) for i, j in up]

    emb = embeddings.reshape(rows, width)
    emb_p = lax.ppermute(emb, "grid", up)
    emb_n = lax.ppermute(emb, "grid", down)
    first = place * blocks
    slots = (adjacent_blocks - first + R_BLK).reshape(-1)
    readout = jnp.pad(readout_matrix, ((0, 0), (0, LANES - channels)))
    truth = jnp.pad(reference_analysis, ((0, LANES - channels), (0, 0))).T
    phase = (zonal_strip.astype(F32) + 0.5) * (math.pi / NLAT) - 0.5 * math.pi
    weight = jnp.cos(phase) * (1.0 + continent_indicator.astype(F32))
    weight = jnp.broadcast_to(weight[:, None], (points, LANES))
    round_of = (jnp.arange(LANES, dtype=jnp.int32) + place) % rounds
    own_ids = ens * members + jnp.arange(members, dtype=jnp.int32)
    own_pick = (jnp.arange(count, dtype=jnp.int32)[None, :] == own_ids[:, None]).astype(jnp.int32)
    own_partners = jnp.sum(companion_matrix[None] * own_pick[:, None, :], axis=-1)
    partner = jnp.zeros((members, LANES), jnp.int32)
    for r in range(rounds):
        partner = jnp.where(round_of[None, :] == r, own_partners[:, r : r + 1], partner)
    partner = jnp.concatenate(
        [partner, jnp.full((8 - members, LANES), channels, jnp.int32)], axis=0
    )

    q, kv = call(
        own_projection, [((rows, width), BF), ((rows, 2 * width), BF)],
        [emb, attention_matrix], name="own_projection",
    )
    adjacent, q = lax.optimization_barrier((adjacent_blocks, q))
    adj_p = lax.ppermute(adjacent, "grid", up)
    adj_n = lax.ppermute(adjacent, "grid", down)
    to_p = jnp.where(place > 0, adj_p[:, 2] - first, -1)
    to_n = jnp.where(place < size - 1, adj_n[:, 1] - first, -1)
    targets = jnp.concatenate([to_p, to_n])
    targets = jnp.where((targets >= 0) & (targets < blocks), targets, -1)
    ids = jnp.stack([jnp.int32(channels), ens % 2 * 16 + place // 4]).astype(jnp.int32)
    emb_p, emb_n, targets, ids, readout, truth, weight, partner = lax.optimization_barrier(
        (emb_p, emb_n, targets, ids, readout, truth, weight, partner)
    )
    kvx, state, send, lse, forecast = call(
        forward,
        [
            ((members, 3 * points, 2 * width), BF),
            ((rows, width), F32),
            ((rows, width + LANES), BF),
            ((rows, LANES), F32),
            ((rows, LANES), F32),
        ],
        [slots, emb_p, emb_n, emb, q, kv, attention_matrix, readout],
        smem=1, name="forward",
    )
    every = lax.all_gather(forecast, "ens", axis=0, tiled=True)
    every, send = lax.optimization_barrier((every, send))
    grad, total = call(
        loss, [((rows, LANES), BF), ((8, LANES), F32)],
        [forecast, every, truth, weight, partner], name="loss",
    )
    grad_p = lax.ppermute(grad, "grid", up)
    grad_n = lax.ppermute(grad, "grid", down)
    got_p = lax.ppermute(send, "grid", up)
    got_n = lax.ppermute(send, "grid", down)
    grad_state, dec, dv = call(
        own_values,
        [((rows, width), F32), ((width, LANES), BF), ((members, points, width), F32)],
        [slots, ids, grad, state, readout, q, kvx, lse, total],
        smem=2,
        scratch=[pltpu.VMEM((members, 3 * points, width), F32)],
        name="own_values",
    )
    (q_halo,) = call(
        halo_query, [((2 * rows, width), BF)], [emb_p, emb_n, attention_matrix], name="halo_query"
    )
    got_p, got_n, grad_p, grad_n, q_halo, dv = lax.optimization_barrier(
        (got_p, got_n, grad_p, grad_n, q_halo, dv)
    )
    go, grad_v, parts = call(
        halo_values,
        [((2 * rows, width), BF), ((rows, width), BF), ((width, width + LANES), BF)],
        [targets, emb_p, emb_n, got_p, got_n, grad_p, grad_n, q_halo, kvx, readout, dv, emb, dec],
        smem=1,
        scratch=[pltpu.VMEM((members, points, width), F32)],
        name="halo_values",
    )
    pieces, got = scatter_start(parts, flat, "co")
    sums = scatter_end(pieces, got, flat, "co").astype(BF)
    pieces, got = scatter_start(sums, flat, "x")
    grad_q, grad_k = call(
        score_backward,
        [((rows, width), BF), ((rows, width), BF)],
        [slots, targets, grad_state, q, kvx, lse, got_p, got_n, q_halo, go],
        smem=2,
        scratch=[pltpu.VMEM((members, 3 * points, width), F32)],
        name="score_backward",
    )
    got, grad_q = lax.optimization_barrier((got, grad_q))
    sums = scatter_end(pieces, got, flat, "x").astype(BF)
    pieces, got = scatter_start(sums, flat, "y")
    (sensitivity,) = call(
        input_gradient, [((rows, width), F32)],
        [emb, grad_q, grad_k, grad_v, attention_matrix, grad_state], name="input_gradient",
    )
    got, sensitivity = lax.optimization_barrier((got, sensitivity))
    sums = scatter_end(pieces, got, flat, "y")
    for axis in ("zh", "zl"):
        pieces, got = scatter_start(sums, flat, axis)
        sums = scatter_end(pieces, got, flat, axis)
    energy = jnp.sum(sums[:, width + channels :]) / (
        count * channels * size * (points // SCORED_ENTRIES)
    )
    return (
        energy,
        sensitivity.reshape(members, points, width),
        sums[:, :width].reshape(-1),
        sums[:, width : width + channels].reshape(-1),
    )


def solution(mesh):
    in_specs = (
        P("ens", "grid", None),
        P(None, "grid"),
        P(),
        P(),
        P("grid", None),
        P(),
        P("grid"),
        P("grid"),
    )
    out_specs = (P(), P("ens", "grid", None), P(("ens", "grid")), P(("ens", "grid")))
    return jax.shard_map(
        per_device, mesh=mesh, in_specs=in_specs, out_specs=out_specs, check_vma=False
    )
```
